32 devices in a mesh: expert: 8 (over z, core), ctx: 4 (over y, x).
Axes of the slice: x: 2, y: 2, z: 4, core: 2. Of those that a mesh axis runs over, the one named last changes fastest.
Arguments:
- query_latent: bfloat16 [1024, 128, 512], P('ctx', 'expert'), may hold values from -3 to 3
- query_rope: bfloat16 [1024, 8192], P('ctx', 'expert'), may hold values from -128 to 128
- latent_cache: bfloat16 [576, 1024], P(None, 'ctx'), may hold values from -32 to 32
- group_order: int32 [4], replicated, may hold values from 0 to 3, each once
Outputs:
- attention_out: bfloat16 [1024, 128, 512], P('ctx', 'expert')
The draws below stay inside these ranges and needn't reach their ends.
Inputs may be any that keep to these rules, and one draw needn't show every extreme that they name: `group_order`: each block index appears once.
All inputs are finite; a program needn't handle non-finite values.
Results may differ from the reference program's by a relative error of at most 0.0045.
Values may be sent and summed in bfloat16 or wider, within the bound.
A program may use at most 64 MiB of HBM per device.

```python
import jax
import jax.numpy as jnp
from jax import lax

HEADS = 128
LATENT = 512
ROPE = 64
GROUP = 256
SEQ = 1024
N_CTX = 4


def attention_draw(key):
    folded = jax.random.fold_in(key, 7001)
    key_one, key_two, key_three = jax.random.split(folded, 3)
    latent_q = 0.5 * jnp.clip(jax.random.normal(key_one, (SEQ, HEADS, LATENT), jnp.float32), -6.0, 6.0)
    rope_q = 0.5 * jnp.clip(jax.random.normal(key_two, (SEQ, HEADS * ROPE), jnp.float32), -6.0, 6.0)
    keys_all = jnp.clip(jax.random.normal(key_three, (LATENT + ROPE, SEQ), jnp.float32), -6.0, 6.0)
    return (latent_q, rope_q, keys_all)


def draw_query_latent(key, part):
    return attention_draw(key)[0].astype(jnp.bfloat16)


def draw_query_rope(key, part):
    return attention_draw(key)[1].astype(jnp.bfloat16)


def draw_latent_cache(key, part):
    return attention_draw(key)[2].astype(jnp.bfloat16)


def setup_inputs(seed: int = 0) -> dict:
    splits = jax.random.split(jax.random.key(seed), 5)
    query_latent = draw_query_latent(jax.random.fold_in(splits[4], 71), 0)
    query_rope = draw_query_rope(jax.random.fold_in(splits[4], 71), 0)
    latent_cache = draw_latent_cache(jax.random.fold_in(splits[4], 71), 0)
    group_order = jax.random.permutation(splits[3], N_CTX).astype(jnp.int32)
    return {"query_latent": query_latent, "query_rope": query_rope, "latent_cache": latent_cache, "group_order": group_order}


score_scale = 192.0 ** -0.5


def attention_reference(query_latent, query_rope, latent_cache, group_order):
    seq_total = latent_cache.shape[1]
    indices = jnp.arange(seq_total, dtype=jnp.int32)
    positions = jnp.take(group_order, indices // GROUP) * GROUP + indices % GROUP
    latent_keys = latent_cache[:LATENT].astype(jnp.float32)
    rope_keys = latent_cache[LATENT:].astype(jnp.float32)
    blocks = seq_total // GROUP
    latent_blocks = query_latent.reshape(blocks, GROUP, HEADS, LATENT)
    rope_blocks = query_rope.reshape(blocks, GROUP, HEADS, ROPE)
    position_blocks = positions.reshape(blocks, GROUP)

    def one_block(inputs):
        latent_block, rope_block, position_block = inputs
        scores = jnp.einsum("qhd,dk->qhk", latent_block.astype(jnp.float32), latent_keys, precision=lax.Precision.HIGHEST)
        scores = scores + jnp.einsum("qhr,rk->qhk", rope_block.astype(jnp.float32), rope_keys, precision=lax.Precision.HIGHEST)
        visible = (positions[None, :] <= position_block[:, None])[:, None, :]
        scores = jnp.where(visible, scores * score_scale, -1e30)
        peak = jnp.max(scores, axis=-1, keepdims=True)
        exponent = jnp.where(visible, jnp.exp(scores - peak), 0.0)
        total = jnp.sum(exponent, axis=-1)
        weights = lax.optimization_barrier(exponent.astype(jnp.bfloat16)).astype(jnp.float32)
        numer = jnp.einsum("qhk,dk->qhd", weights, latent_keys, precision=lax.Precision.HIGHEST)
        return (numer / total[..., None]).astype(jnp.bfloat16)

    outputs = lax.map(one_block, (latent_blocks, rope_blocks, position_blocks))
    return outputs.reshape(seq_total, HEADS, LATENT)


def reference(query_latent, query_rope, latent_cache, group_order):
    return attention_reference(query_latent, query_rope, latent_cache, group_order)
```

```python
import functools

import jax
import jax.numpy as jnp
from jax import lax
from jax.experimental import pallas as pl
from jax.experimental.pallas import tpu as pltpu
from jax.sharding import PartitionSpec as P

MESH = pl.DeviceIdType.MESH
exp_scale = (192.0 ** -0.5) * 1.4426950408889634
far_below = -1e30
SUB = 512
CHUNK = 3


def peer_of(c, d, n, sign):
    if n & (n - 1):
        return lax.rem(c + sign * d + n, n)
    out = c
    bit = 1
    while bit <= d:
        if d & bit:
            out = out + bit - 2 * bit * lax.rem(c // bit, 2)
        bit *= 2
    return out


def kernel(
    n, heads, latent, rope_w, order_ref, q_ref, rope_ref, lat_ref, out_ref,
    qcat, ropes, kv, vt, m_s, l_s, acc_s, s_a, s_b,
    q_sem, own_sem, send_sem, recv_sem, fsend_sem, frecv_sem,
):
    c = lax.axis_index("ctx")
    e = lax.axis_index("expert")
    sib = e + 1 - 2 * lax.rem(e, 2)
    rows = q_ref.shape[0]
    width, keys = lat_ref.shape
    depth = kv.shape[1]
    half = width // 2
    mine = pl.multiple_of(lax.rem(e, 2) * half, 16)
    tiles = rows // SUB

    barrier = pltpu.get_barrier_semaphore()
    for d in range(1, n):
        pl.semaphore_signal(
            barrier, inc=1, device_id={"ctx": peer_of(c, d, n, 1)}, device_id_type=MESH
        )
    pl.semaphore_signal(barrier, inc=1, device_id={"expert": sib}, device_id_type=MESH)

    own = pltpu.make_async_copy(lat_ref, kv.at[0, pl.ds(0, width)], own_sem)
    own.start()
    q_copies = []
    for i in range(4):
        part = pl.ds(i * (rows // 4), rows // 4)
        cp = pltpu.make_async_copy(
            q_ref.at[part], qcat.at[part, pl.ds(0, latent)], q_sem.at[i]
        )
        cp.start()
        q_copies.append(cp)

    here = order_ref[c]
    extra = depth - width
    first_row = lax.broadcasted_iota(jnp.int32, (extra, keys), 0) == 0
    for d in range(n):
        if d == 0:
            bias = jnp.zeros((extra, keys), jnp.float32)
        else:
            seen = order_ref[peer_of(c, d, n, -1)] < here
            bias = jnp.where(first_row, jnp.where(seen, 0.0, far_below), 0.0)
        kv[d, pl.ds(width, extra), :] = bias.astype(jnp.bfloat16)

    lane = lax.broadcasted_iota(jnp.int32, (rows // heads, 128), 1)
    pair = 128 // rope_w
    tail = jnp.where(lane == rope_w, 1.0, 0.0)
    def place(h):
        x = rope_ref[:, pl.ds((h // pair) * 128, 128)].astype(jnp.float32)
        if h % pair:
            x = pltpu.roll(x, 128 - (h % pair) * rope_w, 1)
        ropes[pl.ds(h, rows // heads, stride=heads), :] = jnp.where(lane < rope_w, x, tail)

    for h in range(heads // 2):
        place(h)

    pl.semaphore_wait(barrier, n)
    sends = {}
    for d in range(1, n):
        cp = pltpu.make_async_remote_copy(
            src_ref=lat_ref.at[pl.ds(mine, half)],
            dst_ref=kv.at[d, pl.ds(mine, half)],
            send_sem=send_sem.at[d],
            recv_sem=recv_sem.at[d],
            device_id={"ctx": peer_of(c, d, n, 1)},
            device_id_type=MESH,
        )
        cp.start()
        sends[d] = cp

    for h in range(heads // 2, heads):
        place(h)

    own.wait()
    vt[pl.ds(0, keys), :] = kv[0, pl.ds(0, latent), :].T
    for cp in q_copies:
        cp.wait()

    def fill_rope(i, carry):
        r = pl.ds(pl.multiple_of(i * SUB, SUB), SUB)
        qcat[r, pl.ds(latent, 128)] = ropes[r, :].astype(jnp.bfloat16)
        return carry

    lax.fori_loop(0, tiles, fill_rope, 0)

    def rows_of(i):
        return pl.ds(pl.multiple_of(i * SUB, SUB), SUB)

    def score(i, buf, ds, begin=0):
        r = rows_of(i)
        for k, d in enumerate(ds, begin):
            buf[:, pl.ds(k * keys, keys)] = jnp.dot(
                qcat[r, :], kv[d], preferred_element_type=jnp.float32
            )

    def finish(i, buf, ds, first, last):
        r = rows_of(i)
        ss = [buf[:, pl.ds(k * keys, keys)] for k in range(len(ds))]
        if first:
            sub_rows = lax.broadcasted_iota(jnp.int32, (SUB, keys), 0) // heads
            sub_cols = lax.broadcasted_iota(jnp.int32, (SUB, keys), 1)
            seen = sub_cols - sub_rows <= i * (SUB // heads)
            ss = [jnp.where(seen, ss[0], far_below)]
        m = jnp.max(functools.reduce(jnp.maximum, ss), axis=1, keepdims=True)
        if not first:
            old = m_s[r, :][:, :1]
            m = jnp.maximum(old, m)
            alpha = jnp.exp2((old - m) * exp_scale)
        weights = []
        total = None if first else l_s[r, :] * alpha
        for s in ss:
            p = jnp.exp2((s - m) * exp_scale)
            for k in range(keys // 128):
                part = p[:, k * 128:(k + 1) * 128]
                total = part if total is None else total + part
            weights.append(p.astype(jnp.bfloat16))
        acc = jnp.dot(
            jnp.concatenate(weights, axis=1) if len(ds) > 1 else weights[0],
            vt[pl.ds(ds[0] * keys, len(ds) * keys), :],
            preferred_element_type=jnp.float32,
        )
        if not first:
            acc = acc_s[r, :] * alpha + acc
        if last:
            inv = 1.0 / jnp.sum(total, axis=1, keepdims=True)
            out_ref[r, :] = (acc * inv).astype(jnp.bfloat16)
        else:
            m_s[r, :] = jnp.broadcast_to(m, (SUB, 128))
            l_s[r, :] = total
            acc_s[r, :] = acc

    def phase(ds, first, last, arrive, middle):
        score(0, s_a, ds[:-1])
        arrive()
        score(0, s_a, ds[-1:], len(ds) - 1)

        def step(k, carry):
            i = 2 * k
            score(i + 1, s_b, ds)
            finish(i, s_a, ds, first, last)
            score(i + 2, s_a, ds)
            finish(i + 1, s_b, ds, first, last)
            return carry

        lax.fori_loop(0, tiles // 2 - 1, step, 0)
        middle()
        score(tiles - 1, s_b, ds)
        finish(tiles - 2, s_a, ds, first, last)
        finish(tiles - 1, s_b, ds, first, last)

    def forward(d):
        sends[d].wait_recv()
        cp = pltpu.make_async_remote_copy(
            src_ref=kv.at[d, pl.ds(mine, half)],
            dst_ref=kv.at[d, pl.ds(mine, half)],
            send_sem=fsend_sem.at[d],
            recv_sem=frecv_sem.at[d],
            device_id={"expert": sib},
            device_id_type=MESH,
        )
        cp.start()
        return cp

    groups = [list(range(1, n))[g:g + CHUNK] for g in range(0, n - 1, CHUNK)]
    forwards = {}

    def forward_all(ds):
        for d in ds:
            forwards[d] = forward(d)

    def take(d):
        forwards[d].wait_recv()
        vt[pl.ds(d * keys, keys), :] = kv[d, pl.ds(0, latent), :].T

    phase([0], True, n == 1, lambda: None, lambda: forward_all(groups[0][:-1] if groups else []))
    for g, ds in enumerate(groups):
        last = g == len(groups) - 1
        after = [] if last else groups[g + 1][:-1]
        forward_all(ds[-1:])
        for d in ds[:-1]:
            take(d)
        phase(
            ds, False, last,
            functools.partial(take, ds[-1]), functools.partial(forward_all, after),
        )
    for d in range(1, n):
        sends[d].wait_send()
        forwards[d].wait_send()


def chunked(n, query_latent, query_rope, latent_cache, group_order):
    t, heads, latent = query_latent.shape
    rows = t * heads
    rope_w = query_rope.shape[1] // heads
    width, keys = latent_cache.shape
    depth = latent + 128
    any_spec = pl.BlockSpec(memory_space=pl.ANY)
    out = pl.pallas_call(
        functools.partial(kernel, n, heads, latent, rope_w),
        out_shape=pltpu.VMEM((rows, latent), jnp.bfloat16),
        in_specs=[
            pl.BlockSpec(memory_space=pltpu.SMEM),
            any_spec,
            pl.BlockSpec(memory_space=pltpu.VMEM),
            any_spec,
        ],
        out_specs=pl.BlockSpec(memory_space=pltpu.VMEM),
        scratch_shapes=[
            pltpu.VMEM((rows, depth), jnp.bfloat16),
            pltpu.VMEM((rows, 128), jnp.float32),
            pltpu.VMEM((n, depth, keys), jnp.bfloat16),
            pltpu.VMEM((n * keys, latent), jnp.bfloat16),
            pltpu.VMEM((rows, 128), jnp.float32),
            pltpu.VMEM((rows, 128), jnp.float32),
            pltpu.VMEM((rows, latent), jnp.float32),
            pltpu.VMEM((SUB, CHUNK * keys), jnp.float32),
            pltpu.VMEM((SUB, CHUNK * keys), jnp.float32),
            pltpu.SemaphoreType.DMA((4,)),
            pltpu.SemaphoreType.DMA,
            pltpu.SemaphoreType.DMA((n,)),
            pltpu.SemaphoreType.DMA((n,)),
            pltpu.SemaphoreType.DMA((n,)),
            pltpu.SemaphoreType.DMA((n,)),
        ],
        compiler_params=pltpu.CompilerParams(
            collective_id=0, has_side_effects=True, vmem_limit_bytes=52 * 1024 * 1024
        ),
    )(group_order, query_latent.reshape(rows, latent), query_rope, latent_cache)
    return out.reshape(t, heads, latent)


SUB_SCORE = 512
SUB_OUT = 256


def score_kernel(
    heads, rope_w, order_ref, q_ref, rope_ref, lat_ref,
    acc_ref, m_ref, l_ref, s_ref, vt_ref,
    qcat, rope_in, ropes, kv, vt_own, s_a, s_b,
    q_sem, own_sem, rope_sem, send_sem, recv_sem, relay_sem, diag_sem, fsend_sem, frecv_sem,
):
    c = lax.axis_index("ctx")
    e = lax.axis_index("expert")
    core = lax.rem(e, 2)
    sib = e + 1 - 2 * core
    rows, latent = acc_ref.shape
    width, keys = lat_ref.shape
    depth = kv.shape[1]
    half = width // 2
    lanes = keys // 2
    tiles = rows // SUB_SCORE
    near = [{"ctx": peer_of(c, d, 4, 1)} for d in (1, 2)]
    other = {"expert": sib}

    barrier = pltpu.get_barrier_semaphore()
    for device in (*near, other):
        pl.semaphore_signal(barrier, inc=1, device_id=device, device_id_type=MESH)

    own = pltpu.make_async_copy(lat_ref, kv.at[0, pl.ds(0, width)], own_sem)
    rope = pltpu.make_async_copy(rope_ref, rope_in, rope_sem)
    rope.start()
    own.start()
    q_copies = []
    for i in range(tiles):
        part = pl.ds(i * SUB_SCORE, SUB_SCORE)
        cp = pltpu.make_async_copy(
            q_ref.at[part], qcat.at[part, pl.ds(0, latent)], q_sem.at[i]
        )
        cp.start()
        q_copies.append(cp)

    pl.semaphore_wait(barrier, 3)

    def remote(src, dst, send, recv, device):
        cp = pltpu.make_async_remote_copy(
            src_ref=src, dst_ref=dst, send_sem=send, recv_sem=recv,
            device_id=device, device_id_type=MESH,
        )
        cp.start()
        return cp

    mine = pl.ds(pl.multiple_of(core * lanes, lanes), lanes)
    side = [pl.ds(0, lanes), pl.ds(lanes, lanes)]
    part = [pl.ds(0, half), pl.ds(half, half)]
    sends = {}
    for turn in range(2):
        for d in range(2):
            k = (d + turn) % 2
            sends[d, turn] = remote(
                lat_ref.at[part[k], mine], kv.at[1, part[k], side[d]],
                send_sem.at[d, turn], recv_sem.at[d, turn], near[d],
            )

    here = order_ref[c]
    extra = depth - width
    first_row = lax.broadcasted_iota(jnp.int32, (extra, lanes), 0) == 0
    kv[0, pl.ds(width, extra), :] = jnp.zeros((extra, keys), jnp.bfloat16)
    for d in range(1, 4):
        seen = order_ref[peer_of(c, d, 4, -1)] < here
        bias = jnp.where(first_row, jnp.where(seen, 0.0, far_below), 0.0).astype(jnp.bfloat16)
        if d < 3:
            kv[1, pl.ds(width, extra), side[d - 1]] = bias
            kv[2, pl.ds(width, extra), side[d - 1]] = bias
        else:
            kv[3, pl.ds(width, extra), side[0]] = bias
            kv[3, pl.ds(width, extra), side[1]] = bias

    rope.wait()
    lane = lax.broadcasted_iota(jnp.int32, (rows // heads, 128), 1)
    pair = 128 // rope_w
    last_lane = jnp.where(lane == rope_w, 1.0, 0.0)
    for h in range(heads):
        x = rope_in[:, pl.ds((h // pair) * 128, 128)].astype(jnp.float32)
        if h % pair:
            x = pltpu.roll(x, 128 - (h % pair) * rope_w, 1)
        ropes[pl.ds(h, rows // heads, stride=heads), :] = jnp.where(lane < rope_w, x, last_lane)
    own.wait()
    vt_own[...] = kv[0, pl.ds(0, latent), :].T

    def rows_of(i):
        return pl.ds(i * SUB_SCORE, SUB_SCORE)

    bufs = [s_a, s_b]

    def own_score(i):
        r = rows_of(i)
        qcat[r, pl.ds(latent, 128)] = ropes[r, :].astype(jnp.bfloat16)
        bufs[i % 2][...] = jnp.dot(qcat[r, :], kv[0], preferred_element_type=jnp.float32)

    def own_finish(i):
        r = rows_of(i)
        shape = (SUB_SCORE, keys)
        sub_rows = lax.broadcasted_iota(jnp.int32, shape, 0) // heads
        sub_cols = lax.broadcasted_iota(jnp.int32, shape, 1)
        seen = sub_cols - sub_rows <= i * (SUB_SCORE // heads)
        s = jnp.where(seen, bufs[i % 2][...], far_below)
        m = jnp.max(s, axis=1, keepdims=True)
        p = jnp.exp2((s - m) * exp_scale)
        m_ref[r, :] = jnp.broadcast_to(m, (SUB_SCORE, 128))
        l_ref[r, :] = functools.reduce(
            jnp.add, [p[:, k:k + 128] for k in range(0, keys, 128)]
        )
        acc_ref[r, :] = jnp.dot(
            p.astype(jnp.bfloat16), vt_own[...], preferred_element_type=jnp.float32
        )

    def relay(d):
        sends[d, 0].wait_recv()
        return remote(
            kv.at[1, part[d], side[d]], kv.at[3, part[d], side[0]],
            relay_sem.at[d], diag_sem.at[d], near[1 - d],
        )

    for cp in q_copies[:2]:
        cp.wait()
    own_score(0)
    relays = []
    for i in range(tiles):
        if i + 1 < tiles:
            if i % 2 and i + 2 < tiles:
                q_copies[i + 1].wait()
                q_copies[i + 2].wait()
            elif i % 2:
                q_copies[i + 1].wait()
            own_score(i + 1)
        own_finish(i)
        if i == tiles - 3:
            relays = [relay(0), relay(1)]

    def scores(t):
        def step(k, carry):
            for u in range(4):
                r = pl.ds(pl.multiple_of((4 * k + u) * SUB_SCORE, SUB_SCORE), SUB_SCORE)
                s_ref[r, pl.ds((t - 1) * keys, keys)] = jnp.dot(
                    qcat[r, :], kv[t], preferred_element_type=jnp.float32
                )
            cols = pl.ds(pl.multiple_of(k * (latent // 2), latent // 2), latent // 2)
            vt_ref[pl.ds((t - 1) * keys, keys), cols] = kv[t, cols, :].T
            return carry

        lax.fori_loop(0, 2, step, 0)

    for d in range(2):
        sends[d, 1].wait_recv()
    full = pl.ds(0, width)
    forwards = [remote(kv.at[1, full], kv.at[2, full], fsend_sem.at[0], frecv_sem.at[0], other)]
    scores(1)
    for d in range(2):
        relays[d].wait_recv()
    forwards.append(remote(
        kv.at[3, full, side[0]], kv.at[3, full, side[1]], fsend_sem.at[1], frecv_sem.at[1], other
    ))
    forwards[0].wait_recv()
    scores(2)
    forwards[1].wait_recv()
    scores(3)
    for cp in (*sends.values(), *relays, *forwards):
        cp.wait_send()


def out_kernel(acc_ref, m_ref, l_ref, s_ref, vt_ref, out_ref, done, sems):
    rows = acc_ref.shape[0]
    copies = []
    for i in range(rows // SUB_OUT):
        r = pl.ds(i * SUB_OUT, SUB_OUT)
        ss = [s_ref[r, k:k + 128] for k in range(0, s_ref.shape[1], 128)]
        old = m_ref[r, :]
        m = jnp.max(functools.reduce(jnp.maximum, [old, *ss]), axis=1, keepdims=True)
        alpha = jnp.exp2((old[:, :1] - m) * exp_scale)
        total = l_ref[r, :] * alpha
        weights = []
        for s in ss:
            p = jnp.exp2((s - m) * exp_scale)
            total = total + p
            weights.append(p.astype(jnp.bfloat16))
        acc = jnp.dot(
            jnp.concatenate(weights, axis=1), vt_ref[...], preferred_element_type=jnp.float32
        )
        acc = acc_ref[r, :] * alpha + acc
        inv = 1.0 / jnp.sum(total, axis=1, keepdims=True)
        done[r, :] = (acc * inv).astype(jnp.bfloat16)
        cp = pltpu.make_async_copy(done.at[r], out_ref.at[r], sems.at[i])
        cp.start()
        copies.append(cp)
    for cp in copies:
        cp.wait()


def square(query_latent, query_rope, latent_cache, group_order):
    t, heads, latent = query_latent.shape
    rows = t * heads
    rope_w = query_rope.shape[1] // heads
    width, keys = latent_cache.shape
    depth = latent + 128
    f32, bf16 = jnp.float32, jnp.bfloat16
    hbm_spec = pl.BlockSpec(memory_space=pltpu.HBM)
    vmem_spec = pl.BlockSpec(memory_space=pltpu.VMEM)
    dma = pltpu.SemaphoreType.DMA
    partial = pl.pallas_call(
        functools.partial(score_kernel, heads, rope_w),
        out_shape=[
            pltpu.VMEM((rows, latent), f32),
            pltpu.VMEM((rows, 128), f32),
            pltpu.VMEM((rows, 128), f32),
            pltpu.VMEM((rows, 3 * keys), f32),
            pltpu.VMEM((3 * keys, latent), bf16),
        ],
        in_specs=[pl.BlockSpec(memory_space=pltpu.SMEM), hbm_spec, hbm_spec, hbm_spec],
        out_specs=[vmem_spec] * 5,
        scratch_shapes=[
            pltpu.VMEM((rows, depth), bf16),
            pltpu.VMEM(query_rope.shape, bf16),
            pltpu.VMEM((rows, 128), f32),
            pltpu.VMEM((4, depth, keys), bf16),
            pltpu.VMEM((keys, latent), bf16),
            pltpu.VMEM((SUB_SCORE, keys), f32),
            pltpu.VMEM((SUB_SCORE, keys), f32),
            dma((rows // SUB_SCORE,)), dma, dma,
            dma((2, 2)), dma((2, 2)), dma((2,)), dma((2,)), dma((2,)), dma((2,)),
        ],
        compiler_params=pltpu.CompilerParams(
            collective_id=0, has_side_effects=True, vmem_limit_bytes=30 * 1024 * 1024
        ),
    )(group_order, query_latent.reshape(rows, latent), query_rope, latent_cache)
    out = pl.pallas_call(
        out_kernel,
        out_shape=jax.ShapeDtypeStruct((rows, latent), bf16),
        in_specs=[vmem_spec] * 5,
        out_specs=hbm_spec,
        scratch_shapes=[pltpu.VMEM((rows, latent), bf16), dma((rows // SUB_OUT,))],
        compiler_params=pltpu.CompilerParams(vmem_limit_bytes=12 * 1024 * 1024),
    )(*partial)
    return out.reshape(t, heads, latent)


def body(n, *args):
    return square(*args) if n == 4 else chunked(n, *args)


def solution(mesh):
    placed = (P("ctx", "expert", None), P("ctx", "expert"), P(None, "ctx"), P())
    return jax.shard_map(
        functools.partial(body, mesh.shape["ctx"]),
        mesh=mesh, in_specs=placed, out_specs=P("ctx", "expert", None), check_vma=False,
    )
```

```python
import functools

import jax
import jax.numpy as jnp
from jax import lax
from jax.experimental import pallas as pl
from jax.experimental.pallas import tpu as pltpu
from jax.sharding import PartitionSpec as P

MESH = pl.DeviceIdType.MESH
exp_scale = (192.0 ** -0.5) * 1.4426950408889634
far_below = -1e30
SUB = 512
CHUNK = 3


def peer_of(c, d, n, sign):
    if n & (n - 1):
        return lax.rem(c + sign * d + n, n)
    out = c
    bit = 1
    while bit <= d:
        if d & bit:
            out = out + bit - 2 * bit * lax.rem(c // bit, 2)
        bit *= 2
    return out


def kernel(
    n, heads, latent, rope_w, order_ref, q_ref, rope_ref, lat_ref, out_ref,
    qcat, ropes, kv, vt, m_s, l_s, acc_s, s_a, s_b,
    q_sem, own_sem, send_sem, recv_sem, fsend_sem, frecv_sem,
):
    c = lax.axis_index("ctx")
    e = lax.axis_index("expert")
    sib = e + 1 - 2 * lax.rem(e, 2)
    rows = q_ref.shape[0]
    width, keys = lat_ref.shape
    depth = kv.shape[1]
    half = width // 2
    mine = pl.multiple_of(lax.rem(e, 2) * half, 16)
    tiles = rows // SUB

    barrier = pltpu.get_barrier_semaphore()
    for d in range(1, n):
        pl.semaphore_signal(
            barrier, inc=1, device_id={"ctx": peer_of(c, d, n, 1)}, device_id_type=MESH
        )
    pl.semaphore_signal(barrier, inc=1, device_id={"expert": sib}, device_id_type=MESH)

    own = pltpu.make_async_copy(lat_ref, kv.at[0, pl.ds(0, width)], own_sem)
    own.start()
    q_copies = []
    for i in range(4):
        part = pl.ds(i * (rows // 4), rows // 4)
        cp = pltpu.make_async_copy(
            q_ref.at[part], qcat.at[part, pl.ds(0, latent)], q_sem.at[i]
        )
        cp.start()
        q_copies.append(cp)

    here = order_ref[c]
    extra = depth - width
    first_row = lax.broadcasted_iota(jnp.int32, (extra, keys), 0) == 0
    for d in range(n):
        if d == 0:
            bias = jnp.zeros((extra, keys), jnp.float32)
        else:
            seen = order_ref[peer_of(c, d, n, -1)] < here
            bias = jnp.where(first_row, jnp.where(seen, 0.0, far_below), 0.0)
        kv[d, pl.ds(width, extra), :] = bias.astype(jnp.bfloat16)

    lane = lax.broadcasted_iota(jnp.int32, (rows // heads, 128), 1)
    pair = 128 // rope_w
    tail = jnp.where(lane == rope_w, 1.0, 0.0)
    def place(h):
        x = rope_ref[:, pl.ds((h // pair) * 128, 128)].astype(jnp.float32)
        if h % pair:
            x = pltpu.roll(x, 128 - (h % pair) * rope_w, 1)
        ropes[pl.ds(h, rows // heads, stride=heads), :] = jnp.where(lane < rope_w, x, tail)

    for h in range(heads // 2):
        place(h)

    pl.semaphore_wait(barrier, n)
    sends = {}
    for d in range(1, n):
        cp = pltpu.make_async_remote_copy(
            src_ref=lat_ref.at[pl.ds(mine, half)],
            dst_ref=kv.at[d, pl.ds(mine, half)],
            send_sem=send_sem.at[d],
            recv_sem=recv_sem.at[d],
            device_id={"ctx": peer_of(c, d, n, 1)},
            device_id_type=MESH,
        )
        cp.start()
        sends[d] = cp

    for h in range(heads // 2, heads):
        place(h)

    own.wait()
    vt[pl.ds(0, keys), :] = kv[0, pl.ds(0, latent), :].T
    for cp in q_copies:
        cp.wait()

    def fill_rope(i, carry):
        r = pl.ds(pl.multiple_of(i * SUB, SUB), SUB)
        qcat[r, pl.ds(latent, 128)] = ropes[r, :].astype(jnp.bfloat16)
        return carry

    lax.fori_loop(0, tiles, fill_rope, 0)

    def rows_of(i):
        return pl.ds(pl.multiple_of(i * SUB, SUB), SUB)

    def score(i, buf, ds, begin=0):
        r = rows_of(i)
        for k, d in enumerate(ds, begin):
            buf[:, pl.ds(k * keys, keys)] = jnp.dot(
                qcat[r, :], kv[d], preferred_element_type=jnp.float32
            )

    def finish(i, buf, ds, first, last):
        r = rows_of(i)
        ss = [buf[:, pl.ds(k * keys, keys)] for k in range(len(ds))]
        if first:
            sub_rows = lax.broadcasted_iota(jnp.int32, (SUB, keys), 0) // heads
            sub_cols = lax.broadcasted_iota(jnp.int32, (SUB, keys), 1)
            seen = sub_cols - sub_rows <= i * (SUB // heads)
            ss = [jnp.where(seen, ss[0], far_below)]
        m = jnp.max(functools.reduce(jnp.maximum, ss), axis=1, keepdims=True)
        if not first:
            old = m_s[r, :][:, :1]
            m = jnp.maximum(old, m)
            alpha = jnp.exp2((old - m) * exp_scale)
        weights = []
        total = None if first else l_s[r, :] * alpha
        for s in ss:
            p = jnp.exp2((s - m) * exp_scale)
            for k in range(keys // 128):
                part = p[:, k * 128:(k + 1) * 128]
                total = part if total is None else total + part
            weights.append(p.astype(jnp.bfloat16))
        acc = jnp.dot(
            jnp.concatenate(weights, axis=1) if len(ds) > 1 else weights[0],
            vt[pl.ds(ds[0] * keys, len(ds) * keys), :],
            preferred_element_type=jnp.float32,
        )
        if not first:
            acc = acc_s[r, :] * alpha + acc
        if last:
            inv = 1.0 / jnp.sum(total, axis=1, keepdims=True)
            out_ref[r, :] = (acc * inv).astype(jnp.bfloat16)
        else:
            m_s[r, :] = jnp.broadcast_to(m, (SUB, 128))
            l_s[r, :] = total
            acc_s[r, :] = acc

    def phase(ds, first, last, arrive, middle):
        score(0, s_a, ds[:-1])
        arrive()
        score(0, s_a, ds[-1:], len(ds) - 1)

        def step(k, carry):
            i = 2 * k
            score(i + 1, s_b, ds)
            finish(i, s_a, ds, first, last)
            score(i + 2, s_a, ds)
            finish(i + 1, s_b, ds, first, last)
            return carry

        lax.fori_loop(0, tiles // 2 - 1, step, 0)
        middle()
        score(tiles - 1, s_b, ds)
        finish(tiles - 2, s_a, ds, first, last)
        finish(tiles - 1, s_b, ds, first, last)

    def forward(d):
        sends[d].wait_recv()
        cp = pltpu.make_async_remote_copy(
            src_ref=kv.at[d, pl.ds(mine, half)],
            dst_ref=kv.at[d, pl.ds(mine, half)],
            send_sem=fsend_sem.at[d],
            recv_sem=frecv_sem.at[d],
            device_id={"expert": sib},
            device_id_type=MESH,
        )
        cp.start()
        return cp

    groups = [list(range(1, n))[g:g + CHUNK] for g in range(0, n - 1, CHUNK)]
    forwards = {}

    def forward_all(ds):
        for d in ds:
            forwards[d] = forward(d)

    def take(d):
        forwards[d].wait_recv()
        vt[pl.ds(d * keys, keys), :] = kv[d, pl.ds(0, latent), :].T

    phase([0], True, n == 1, lambda: None, lambda: forward_all(groups[0][:-1] if groups else []))
    for g, ds in enumerate(groups):
        last = g == len(groups) - 1
        after = [] if last else groups[g + 1][:-1]
        forward_all(ds[-1:])
        for d in ds[:-1]:
            take(d)
        phase(
            ds, False, last,
            functools.partial(take, ds[-1]), functools.partial(forward_all, after),
        )
    for d in range(1, n):
        sends[d].wait_send()
        forwards[d].wait_send()


def chunked(n, query_latent, query_rope, latent_cache, group_order):
    t, heads, latent = query_latent.shape
    rows = t * heads
    rope_w = query_rope.shape[1] // heads
    width, keys = latent_cache.shape
    depth = latent + 128
    any_spec = pl.BlockSpec(memory_space=pl.ANY)
    out = pl.pallas_call(
        functools.partial(kernel, n, heads, latent, rope_w),
        out_shape=pltpu.VMEM((rows, latent), jnp.bfloat16),
        in_specs=[
            pl.BlockSpec(memory_space=pltpu.SMEM),
            any_spec,
            pl.BlockSpec(memory_space=pltpu.VMEM),
            any_spec,
        ],
        out_specs=pl.BlockSpec(memory_space=pltpu.VMEM),
        scratch_shapes=[
            pltpu.VMEM((rows, depth), jnp.bfloat16),
            pltpu.VMEM((rows, 128), jnp.float32),
            pltpu.VMEM((n, depth, keys), jnp.bfloat16),
            pltpu.VMEM((n * keys, latent), jnp.bfloat16),
            pltpu.VMEM((rows, 128), jnp.float32),
            pltpu.VMEM((rows, 128), jnp.float32),
            pltpu.VMEM((rows, latent), jnp.float32),
            pltpu.VMEM((SUB, CHUNK * keys), jnp.float32),
            pltpu.VMEM((SUB, CHUNK * keys), jnp.float32),
            pltpu.SemaphoreType.DMA((4,)),
            pltpu.SemaphoreType.DMA,
            pltpu.SemaphoreType.DMA((n,)),
            pltpu.SemaphoreType.DMA((n,)),
            pltpu.SemaphoreType.DMA((n,)),
            pltpu.SemaphoreType.DMA((n,)),
        ],
        compiler_params=pltpu.CompilerParams(
            collective_id=0, has_side_effects=True, vmem_limit_bytes=52 * 1024 * 1024
        ),
    )(group_order, query_latent.reshape(rows, latent), query_rope, latent_cache)
    return out.reshape(t, heads, latent)


SUB_SCORE = 512
SUB_OUT = 256


def score_kernel(
    heads, rope_w, order_ref, q_ref, rope_ref, lat_ref,
    acc_ref, m_ref, l_ref, peak_ref, s_ref, vt_ref,
    order, qcat, rope_in, ropes, kv, vt_own, s_a, s_b,
    order_sem, q_sem, own_sem, rope_sem, send_sem, recv_sem, relay_sem, diag_sem, fsend_sem, frecv_sem,
):
    c = lax.axis_index("ctx")
    e = lax.axis_index("expert")
    core = lax.rem(e, 2)
    sib = e + 1 - 2 * core
    rows, latent = acc_ref.shape
    width, keys = lat_ref.shape
    depth = kv.shape[1]
    half = width // 2
    lanes = keys // 2
    tiles = rows // SUB_SCORE
    near = [{"ctx": peer_of(c, d, 4, 1)} for d in (1, 2)]
    other = {"expert": sib}

    barrier = pltpu.get_barrier_semaphore()
    for device in (*near, other):
        pl.semaphore_signal(barrier, inc=1, device_id=device, device_id_type=MESH)

    places = pltpu.make_async_copy(order_ref, order, order_sem)
    places.start()
    own = pltpu.make_async_copy(lat_ref, kv.at[0, pl.ds(0, width)], own_sem)
    rope = pltpu.make_async_copy(rope_ref, rope_in, rope_sem)
    rope.start()
    own.start()
    q_copies = []
    for i in range(tiles):
        part = pl.ds(i * SUB_SCORE, SUB_SCORE)
        cp = pltpu.make_async_copy(
            q_ref.at[part], qcat.at[part, pl.ds(0, latent)], q_sem.at[i]
        )
        cp.start()
        q_copies.append(cp)

    pl.semaphore_wait(barrier, 3)

    def remote(src, dst, send, recv, device):
        cp = pltpu.make_async_remote_copy(
            src_ref=src, dst_ref=dst, send_sem=send, recv_sem=recv,
            device_id=device, device_id_type=MESH,
        )
        cp.start()
        return cp

    mine = pl.ds(pl.multiple_of(core * lanes, lanes), lanes)
    side = [pl.ds(0, lanes), pl.ds(lanes, lanes)]
    part = [pl.ds(0, half), pl.ds(half, half)]
    sends = {}
    for turn in range(2):
        for d in range(2):
            k = (d + turn) % 2
            sends[d, turn] = remote(
                lat_ref.at[part[k], mine], kv.at[1, part[k], side[d]],
                send_sem.at[d, turn], recv_sem.at[d, turn], near[d],
            )

    places.wait()
    here = order[c]
    extra = depth - width
    first_row = lax.broadcasted_iota(jnp.int32, (extra, lanes), 0) == 0
    kv[0, pl.ds(width, extra), :] = jnp.zeros((extra, keys), jnp.bfloat16)
    for d in range(1, 4):
        seen = order[peer_of(c, d, 4, -1)] < here
        bias = jnp.where(first_row, jnp.where(seen, 0.0, far_below), 0.0).astype(jnp.bfloat16)
        if d < 3:
            kv[1, pl.ds(width, extra), side[d - 1]] = bias
            kv[2, pl.ds(width, extra), side[d - 1]] = bias
        else:
            kv[3, pl.ds(width, extra), side[0]] = bias
            kv[3, pl.ds(width, extra), side[1]] = bias

    rope.wait()
    lane = lax.broadcasted_iota(jnp.int32, (rows // heads, 128), 1)
    pair = 128 // rope_w
    last_lane = jnp.where(lane == rope_w, 1.0, 0.0)
    for h in range(heads):
        x = rope_in[:, pl.ds((h // pair) * 128, 128)].astype(jnp.float32)
        if h % pair:
            x = pltpu.roll(x, 128 - (h % pair) * rope_w, 1)
        ropes[pl.ds(h, rows // heads, stride=heads), :] = jnp.where(lane < rope_w, x, last_lane)
    own.wait()
    vt_own[...] = kv[0, pl.ds(0, latent), :].T

    def rows_of(i):
        return pl.ds(i * SUB_SCORE, SUB_SCORE)

    bufs = [s_a, s_b]

    def own_score(i):
        r = rows_of(i)
        qcat[r, pl.ds(latent, 128)] = ropes[r, :].astype(jnp.bfloat16)
        bufs[i % 2][...] = exp_scale * jnp.dot(
            qcat[r, :], kv[0], preferred_element_type=jnp.float32
        )

    def own_finish(i):
        r = rows_of(i)
        shape = (SUB_SCORE, keys)
        sub_rows = lax.broadcasted_iota(jnp.int32, shape, 0) // heads
        sub_cols = lax.broadcasted_iota(jnp.int32, shape, 1)
        seen = sub_cols - sub_rows <= i * (SUB_SCORE // heads)
        s = jnp.where(seen, bufs[i % 2][...], far_below)
        m = jnp.max(s, axis=1, keepdims=True)
        p = jnp.exp2(s - m)
        m_ref[r, :] = jnp.broadcast_to(m, (SUB_SCORE, 128))
        peak_ref[r, :] = jnp.broadcast_to(m, (SUB_SCORE, 128))
        l_ref[r, :] = functools.reduce(
            jnp.add, [p[:, k:k + 128] for k in range(0, keys, 128)]
        )
        acc_ref[r, :] = jnp.dot(
            p.astype(jnp.bfloat16), vt_own[...], preferred_element_type=jnp.float32
        )

    def relay(d):
        sends[d, 0].wait_recv()
        return remote(
            kv.at[1, part[d], side[d]], kv.at[3, part[d], side[0]],
            relay_sem.at[d], diag_sem.at[d], near[1 - d],
        )

    for cp in q_copies[:tiles // 2]:
        cp.wait()
    own_score(0)
    for i in range(tiles):
        if i + 1 == tiles // 2:
            for cp in q_copies[tiles // 2:]:
                cp.wait()
        if i + 1 < tiles:
            own_score(i + 1)
        own_finish(i)
    relays = [relay(0), relay(1)]

    def scores(t):
        for i in range(tiles):
            r = rows_of(i)
            s = exp_scale * jnp.dot(qcat[r, :], kv[t], preferred_element_type=jnp.float32)
            s_ref[r, pl.ds((t - 1) * keys, keys)] = s
            peak_ref[r, :] = functools.reduce(
                jnp.maximum, [s[:, k:k + 128] for k in range(0, keys, 128)], peak_ref[r, :]
            )
        vt_ref[pl.ds((t - 1) * keys, keys), :] = kv[t, pl.ds(0, latent), :].T

    for d in range(2):
        sends[d, 1].wait_recv()
    full = pl.ds(0, width)
    forwards = [remote(kv.at[1, full], kv.at[2, full], fsend_sem.at[0], frecv_sem.at[0], other)]
    scores(1)
    for d in range(2):
        relays[d].wait_recv()
    forwards.append(remote(
        kv.at[3, full, side[0]], kv.at[3, full, side[1]], fsend_sem.at[1], frecv_sem.at[1], other
    ))
    forwards[0].wait_recv()
    scores(2)
    forwards[1].wait_recv()
    scores(3)
    for cp in (*sends.values(), *relays, *forwards):
        cp.wait_send()


def out_kernel(acc_ref, m_ref, l_ref, peak_ref, s_ref, vt_ref, out_ref, done, sems):
    rows = acc_ref.shape[0]
    copies = []
    for i in range(rows // SUB_OUT):
        r = pl.ds(i * SUB_OUT, SUB_OUT)
        ss = [s_ref[r, k:k + 128] for k in range(0, s_ref.shape[1], 128)]
        m = jnp.max(peak_ref[r, :], axis=1, keepdims=True)
        alpha = jnp.exp2(m_ref[r, :] - m)
        total = l_ref[r, :] * alpha
        weights = []
        for s in ss:
            p = jnp.exp2(s - m)
            total = total + p
            weights.append(p.astype(jnp.bfloat16))
        acc = jnp.dot(
            jnp.concatenate(weights, axis=1), vt_ref[...], preferred_element_type=jnp.float32
        )
        inv = 1.0 / jnp.sum(total, axis=1, keepdims=True)
        for k in range(0, acc.shape[1], 128):
            part = acc_ref[r, k:k + 128] * alpha + acc[:, k:k + 128]
            done[r, k:k + 128] = (part * inv).astype(jnp.bfloat16)
        cp = pltpu.make_async_copy(done.at[r], out_ref.at[r], sems.at[i])
        cp.start()
        copies.append(cp)
    for cp in copies:
        cp.wait()


def square(query_latent, query_rope, latent_cache, group_order):
    t, heads, latent = query_latent.shape
    rows = t * heads
    rope_w = query_rope.shape[1] // heads
    width, keys = latent_cache.shape
    depth = latent + 128
    f32, bf16 = jnp.float32, jnp.bfloat16
    hbm_spec = pl.BlockSpec(memory_space=pltpu.HBM)
    vmem_spec = pl.BlockSpec(memory_space=pltpu.VMEM)
    dma = pltpu.SemaphoreType.DMA
    partial = pl.pallas_call(
        functools.partial(score_kernel, heads, rope_w),
        out_shape=[
            pltpu.VMEM((rows, latent), f32),
            pltpu.VMEM((rows, 128), f32),
            pltpu.VMEM((rows, 128), f32),
            pltpu.VMEM((rows, 128), f32),
            pltpu.VMEM((rows, 3 * keys), f32),
            pltpu.VMEM((3 * keys, latent), bf16),
        ],
        in_specs=[hbm_spec] * 4,
        out_specs=[vmem_spec] * 6,
        scratch_shapes=[
            pltpu.SMEM(group_order.shape, jnp.int32),
            pltpu.VMEM((rows, depth), bf16),
            pltpu.VMEM(query_rope.shape, bf16),
            pltpu.VMEM((rows, 128), f32),
            pltpu.VMEM((4, depth, keys), bf16),
            pltpu.VMEM((keys, latent), bf16),
            pltpu.VMEM((SUB_SCORE, keys), f32),
            pltpu.VMEM((SUB_SCORE, keys), f32),
            dma, dma((rows // SUB_SCORE,)), dma, dma,
            dma((2, 2)), dma((2, 2)), dma((2,)), dma((2,)), dma((2,)), dma((2,)),
        ],
        compiler_params=pltpu.CompilerParams(
            collective_id=0, has_side_effects=True, vmem_limit_bytes=28 * 1024 * 1024
        ),
    )(group_order, query_latent.reshape(rows, latent), query_rope, latent_cache)
    out = pl.pallas_call(
        out_kernel,
        out_shape=jax.ShapeDtypeStruct((rows, latent), bf16),
        in_specs=[vmem_spec] * 6,
        out_specs=hbm_spec,
        scratch_shapes=[pltpu.VMEM((rows, latent), bf16), dma((rows // SUB_OUT,))],
        compiler_params=pltpu.CompilerParams(vmem_limit_bytes=12 * 1024 * 1024),
    )(*partial)
    return out.reshape(t, heads, latent)


def body(n, *args):
    return square(*args) if n == 4 else chunked(n, *args)


def solution(mesh):
    placed = (P("ctx", "expert", None), P("ctx", "expert"), P(None, "ctx"), P())
    return jax.shard_map(
        functools.partial(body, mesh.shape["ctx"]),
        mesh=mesh, in_specs=placed, out_specs=P("ctx", "expert", None), check_vma=False,
    )
```
